256 devices in a mesh: section: 16 (over y_hi, x, core), expert: 16 (over z, y_lo).
Axes of the slice: x: 4, y: 4 (y_hi: 2, y_lo: 2; y = y_hi * 2 + y_lo), z: 8, core: 2. Of those that a mesh axis runs over, the one named last changes fastest.
Arguments:
- cotangent: bfloat16 [16, 2048, 4096], P('section', 'expert'), may hold values from -6 to 6
- routes: int32 [16, 2048, 2], P('section', 'expert'), may hold values from 0 to 15, all different within a row; in each aligned block of 64 rows (0 to 63, 64 to 127, ..., all dimensions but the last counted through in order) at most 16 rows name the same one
- gate_prob: float32 [16, 2048, 2], P('section', 'expert'), may hold values from 0.05 to 1
- hidden: bfloat16 [16, 16, 2, 16, 16, 1536], P('section', 'expert'), may hold values from -6 to 6
Outputs:
- grad_pair: bfloat16 [8, 16, 1536, 4096], P(None, 'expert', 'section')
The draws below stay inside these ranges and needn't reach their ends.
Inputs may be any that keep to these rules, and one draw needn't show every extreme that they name: `routes`: each row names 2 different experts. In each aligned block of 64 rows (one micro-batch of one device) no expert is named by more than 16 rows.
All inputs are finite; a program needn't handle non-finite values.
Results may differ from the reference program's by a relative error of at most 0.0059.
Values may be sent and summed in bfloat16 or wider, within the bound.
A program may use at most 128 MiB of HBM per device.

```python
import math
import jax
import jax.numpy as jnp
import numpy as np
from jax import lax

D = 4096
FF = 1536
TOK_MB = 64
MB = 2
TOP = 2
EXPERTS = 16
CAP = 16
TOKENS = 2048
N_SECTION = 16
N_EXPERT = 16


def levels(own_key, dims, cuts, least, top_value):
    gain, own = 1.0, jax.random.fold_in(own_key, 6)
    for dim, parts in cuts:
        heights = jnp.exp(jax.random.uniform(jax.random.fold_in(own, dim), (parts,), jnp.float32, least / len(cuts), top_value / len(cuts)))
        gain = gain * jnp.repeat(heights, dims[dim] // parts).reshape([-1 if axis == dim else 1 for axis in range(len(dims))])
    return gain


def deal_out(key, own, number, rows, count, top, bound, lean):
    sequence = jax.random.permutation(key, count)
    crowded, common = load_shares(count, rows * top, bound, lean, True), load_shares(count, rows * top, bound, lean, False)
    places = jnp.arange(count)

    def named(sizes, turn):
        used = int((sizes > 0).sum())
        fixed = max(1, used // 4)
        passed = fixed + (places - fixed + turn * (used - fixed)) % max(1, count - fixed)
        return jnp.zeros((count,), jnp.int32).at[sequence[jnp.where(places < fixed, places, passed)]].set(jnp.asarray(sizes, jnp.int32))

    sizes = jnp.where(number % 4 == 0, named(crowded, number // 4), named(common, number - number // 4 - 1))
    mixed = jax.random.permutation(jax.random.fold_in(own, 3), count)
    giver, taker = mixed[0:count // 2 * 2:2], mixed[1:count // 2 * 2:2]
    slack = jnp.minimum(sizes[giver] - 1, bound - sizes[taker]) // 2
    slack = jnp.where((giver == sequence[0]) | (taker == sequence[0]) | (sizes[taker] == 0), 0, jnp.maximum(slack, 0))
    passed = jax.random.randint(jax.random.fold_in(own, 4), (count // 2,), 0, 1 << 20) % (slack + 1)
    sizes = sizes.at[giver].add(-passed).at[taker].add(passed)
    members = jnp.searchsorted(jnp.cumsum(sizes), jnp.arange(rows * top), side="right").astype(jnp.int32)
    listing = members.reshape(top, rows).T
    listing = listing[jax.random.permutation(jax.random.fold_in(own, 1), rows)]
    turn = jax.random.randint(jax.random.fold_in(own, 2), (rows, 1), 0, top)
    return jnp.take_along_axis(listing, (jnp.arange(top)[None, :] + turn) % top, axis=1)


def load_shares(amount, total, bound, skew, full):
    portions = [(1 << 20) // math.isqrt(grade ** skew) + 1 for grade in range(1, amount + 1)]
    largest = bound if full else min(bound, max(-(-total // amount), total * portions[0] // sum(portions)))
    least = 1 if total - largest >= amount - 1 else 0
    counts, rest = [largest] + [least] * (amount - 1), total - largest - least * (amount - 1)
    while rest > 0:
        free = [i for i in range(1, amount) if counts[i] < largest] or [i for i in range(1, amount) if counts[i] < bound]
        pool, left = sum([portions[i] for i in free]), rest
        for i in free:
            more = min(bound - counts[i], max(1, left * portions[i] // pool), rest)
            counts[i] = counts[i] + more
            rest = rest - more
    return np.array(counts)


def noise(key, shape, scale, reach, split=(), held_as=jnp.bfloat16):
    drawn = jax.random.normal(key, shape, jnp.float32) * scale
    if len(split) > 0:
        drawn = levels(key, shape, split, -0.22, 0.18) * drawn
    return jnp.clip(drawn, min=-reach, max=reach).astype(held_as)


def setup_inputs(seed: int = 0) -> dict:
    key_list = jax.random.split(jax.random.key(seed), 5)
    cotangent = noise(key_list[0], (N_SECTION, TOKENS, D), 1.0, 6.0, ((0, 16), (1, 16)))
    routes_keys = jax.random.split(jax.random.fold_in(key_list[1], 1), N_SECTION * TOKENS // TOK_MB)
    routes_turns = jax.random.permutation(jax.random.fold_in(key_list[1], 3), N_SECTION * TOKENS // TOK_MB)
    routes = jax.vmap(lambda own, number: deal_out(jax.random.fold_in(key_list[1], 2), own, number, TOK_MB, EXPERTS, TOP, CAP, 2))(routes_keys, routes_turns).reshape((N_SECTION, TOKENS, TOP))
    gate_prob = jnp.clip(jnp.exp(math.log(1.0) - 2.9957323 * jax.random.uniform(key_list[2], (N_SECTION, TOKENS, TOP), jnp.float32) ** levels(key_list[2], (N_SECTION, TOKENS, TOP), ((0, 16), (1, 16)), -0.2, 0.2)), 0.05, 1.0)
    hidden = noise(key_list[3], (N_SECTION, EXPERTS, MB, N_EXPERT, CAP, FF), 1.0, 6.0, ((0, 16), (1, 16)))
    return dict(cotangent=cotangent, routes=routes, gate_prob=gate_prob, hidden=hidden)


def slot_index(route_blk):
    labels = jnp.arange(EXPERTS, dtype=jnp.int32)
    hits = (route_blk[:, :, None] == labels).astype(jnp.int32)
    per_token = lax.optimization_barrier(jnp.sum(hits, axis=1))
    before = jnp.cumsum(per_token, axis=0) - per_token
    return lax.optimization_barrier(jnp.sum(hits * before[:, None, :], axis=2))

def pack_block(cot_blk, route_blk, prob_blk):
    slots = slot_index(route_blk)
    flat = (route_blk * CAP + slots).reshape(-1).astype(jnp.int32)
    weighted = (prob_blk[:, :, None] * cot_blk[:, None, :].astype(jnp.float32)).astype(jnp.bfloat16)
    empty = jnp.zeros((EXPERTS * CAP, D), jnp.bfloat16)
    return empty.at[flat].set(weighted.reshape(-1, D)).reshape(EXPERTS, CAP, D)

def section_grad(cot, route, prob, hid):
    blocks = N_EXPERT * MB
    packed = jax.vmap(pack_block)(cot.reshape(blocks, TOK_MB, D), route.reshape(blocks, TOK_MB, TOP), prob.reshape(blocks, TOK_MB, TOP))
    packed = packed.reshape(N_EXPERT, MB, EXPERTS, CAP, D).transpose(2, 1, 0, 3, 4)

    def one_expert(pair):
        acts, rows = pair
        total = lax.dot_general(acts.reshape(-1, FF), rows.reshape(-1, D), (((0,), (0,)), ((), ())), preferred_element_type=jnp.float32)
        return total.astype(jnp.bfloat16)
    return lax.map(one_expert, (hid, packed))

def reference(cotangent, routes, gate_prob, hidden):

    def pair_sum(index):
        mirror = N_SECTION - 1 - index
        lower = section_grad(cotangent[index], routes[index], gate_prob[index], hidden[index])
        upper = section_grad(cotangent[mirror], routes[mirror], gate_prob[mirror], hidden[mirror])
        return (lower.astype(jnp.float32) + upper.astype(jnp.float32)).astype(jnp.bfloat16)
    return lax.map(pair_sum, jnp.arange(N_SECTION // 2, dtype=jnp.int32))
```

```python
import functools

import jax
import jax.numpy as jnp
from jax import lax
from jax.experimental import pallas as pl
from jax.experimental.pallas import tpu as pltpu
from jax.sharding import PartitionSpec as P

MESH = pl.DeviceIdType.MESH
NZ = 8
CAP = 16
TOK = 128
BLK = 64
SECTIONS = 16
AHEAD = 4
CHUNK = 256
STEPS = (
    (0, 1, 0), (1, 0, 0), (0, 3, 1), (1, 2, 0), (0, 2, 0), (1, 1, 1), (0, 0, 1), (1, 3, 0),
    (0, 1, 1), (1, 0, 1), (0, 3, 0), (1, 2, 1), (0, 2, 1), (1, 1, 0), (1, 3, 1),
)
Z_STEPS = (4, 3, 5, 2, 6, 1, 7)


def drain(ref, sem):
    pltpu.make_async_copy(ref, ref, sem).wait()


def kernel(
    cot, routes, gates, hid, out,
    cotb, rts, gts, sel, gain, packed, arrived, acts, acts_t, result,
    meta_send, meta_recv, cot_send, cot_recv, hid_send, hid_recv, z_send, z_recv, z_own, out_send, out_recv, out_own,
):
    chunks, _, _, width = cotb.shape
    ff = acts.shape[2]
    rows = result.shape[2]
    half = chunks * width
    depth = 2 * acts.shape[1]
    s = lax.axis_index("section")
    e = lax.axis_index("expert")
    y_hi, x, core = s // 8, (s // 2) % 4, s % 2
    z, y_lo = e // 2, e % 2
    chip = s // 2
    base = 2 * chip * (1 - core) + (14 - 2 * chip) * core
    pair = 2 * chip * (1 - chip // 4) + (15 - 2 * chip) * (chip // 4)
    other_e = z * 2 + 1 - y_lo
    partner = 2 * chip + 1 - core
    source = core * 2 + y_lo

    def section_at(step):
        a, b, c = step
        return ((y_hi + a) % 2) * 8 + ((x + b) % 4) * 2 + (core + c) % 2

    barrier = pltpu.get_barrier_semaphore()
    peers = [(section_at(step), e) for step in STEPS]
    peers += [(s, ((z + i) % NZ) * 2 + y_lo) for i in range(1, NZ)]
    peers += [(2 * chip, other_e), (2 * chip + 1, other_e), (14 - 2 * chip, other_e), (15 - 2 * chip, other_e)]
    for peer in peers:
        pl.semaphore_signal(barrier, inc=1, device_id=peer, device_id_type=MESH)
    pl.semaphore_wait(barrier, len(peers))

    def remote(src, dst, send, recv, device):
        pltpu.make_async_remote_copy(
            src_ref=src, dst_ref=dst, send_sem=send, recv_sem=recv, device_id=device, device_id_type=MESH
        ).start()

    targets = [(h, f, (base + h, z * 2 + (y_lo + f) % 2)) for h in range(2) for f in range(2)]

    def each_target(to_other, to_self):
        for i, (h, f, device) in enumerate(targets):
            if i == 0:
                @pl.when(core == 0)
                def _():
                    to_self(h)

                @pl.when(core == 1)
                def _():
                    to_other(i, h, device)
            else:
                to_other(i, h, device)

    def send_meta(i, h, device):
        remote(routes, rts.at[source], meta_send.at[i, 0], meta_recv.at[source, 0], device)
        remote(gates, gts.at[source], meta_send.at[i, 1], meta_recv.at[source, 1], device)

    def keep_meta(h):
        pltpu.make_async_copy(routes, rts.at[source], meta_recv.at[source, 0]).start()
        pltpu.make_async_copy(gates, gts.at[source], meta_recv.at[source, 1]).start()

    def send_rows(n):
        def cut(h):
            return cot.at[:, pl.ds(pl.multiple_of(h * half + n * width, width), width)]

        each_target(
            lambda i, h, device: remote(
                cut(h), cotb.at[n, source], cot_send.at[i], cot_recv.at[n, source], device
            ),
            lambda h: pltpu.make_async_copy(cut(h), cotb.at[n, source], cot_recv.at[n, source]).start(),
        )

    each_target(send_meta, keep_meta)
    send_rows(0)
    send_rows(1)

    block = acts.shape[1] // 2

    @pl.when(core == 0)
    def _():
        pltpu.make_async_copy(hid, acts.at[0], hid_recv.at[0]).start()
        remote(hid, acts.at[0], hid_send.at[0], hid_recv.at[0], (partner, e))

    @pl.when(core == 1)
    def _():
        for b in range(2):
            part = pl.ds(b * block, block)
            remote(hid.at[part], acts.at[1, part], hid_send.at[b], hid_recv.at[1], (base + b, e))

    def rest(n, carry):
        send_rows(n)
        return carry

    lax.fori_loop(2, chunks, rest, 0)

    token = lax.broadcasted_iota(jnp.int32, (TOK, TOK), 1)
    row = lax.broadcasted_iota(jnp.int32, (TOK, TOK), 0)
    earlier = jnp.where((row < token) & ((row >> 6) == (token >> 6)), 1.0, 0.0).astype(jnp.bfloat16)
    place = (row & (CAP - 1)).astype(jnp.float32)
    named = lax.broadcasted_iota(jnp.int32, (NZ, TOK), 0) * 2 + y_lo

    def spread(a):
        return jnp.broadcast_to(a[:, None, :], (NZ, CAP, TOK)).reshape(NZ * CAP, TOK)

    for q in range(4):
        drain(rts.at[q], meta_recv.at[q, 0])
        drain(gts.at[q], meta_recv.at[q, 1])
        first = rts[q, 0:1, :] == named
        second = rts[q, 1:2, :] == named
        hits = jnp.where(first | second, 1.0, 0.0)
        weight = jnp.where(first, gts[q, 0:1, :], 0.0) + jnp.where(second, gts[q, 1:2, :], 0.0)
        before = jnp.dot(hits.astype(jnp.bfloat16), earlier, preferred_element_type=jnp.float32)
        chosen = (spread(hits) > 0.5) & (spread(before) == place)
        weight = spread(weight)
        for b in range(2):
            mine = chosen & ((token >> 6) == b)
            sel[q, b * TOK : (b + 1) * TOK, :] = jnp.where(mine, 1.0, 0.0).astype(jnp.bfloat16)
            total = jnp.sum(jnp.where(mine, weight, 0.0), axis=1, keepdims=True)
            gain[q, b * TOK : (b + 1) * TOK, :] = jnp.broadcast_to(total, (TOK, TOK))

    def pack(n):
        for q in range(4):
            drain(cotb.at[n, q], cot_recv.at[n, q])
            picked = jnp.dot(sel[q], cotb[n, q], preferred_element_type=jnp.float32)
            scale = jnp.concatenate([gain[q]] * (width // TOK), axis=1)
            slots = (picked * scale).astype(jnp.bfloat16).reshape(2, NZ, CAP, width)
            for b in range(2):
                packed[n, :, q // 2, b, (q % 2) * CAP : (q % 2 + 1) * CAP, :] = slots[b]
        for i in Z_STEPS:
            to = (z + i) % NZ
            remote(packed.at[n, to], arrived.at[n, :, :, z], z_send, z_recv.at[n], (s, to * 2 + y_lo))
        pltpu.make_async_copy(packed.at[n, z], arrived.at[n, :, :, z], z_own.at[n]).start()

    def pack_step(n, carry):
        pack(n)
        return carry

    lax.fori_loop(0, AHEAD, pack_step, 0)

    mine = pl.ds(pl.multiple_of(core * block, block), block)
    theirs = pl.ds(pl.multiple_of((1 - core) * block, block), block)
    drain(acts.at[1, mine], hid_recv.at[1])
    remote(acts.at[1, mine], acts.at[1, mine], hid_send.at[2], hid_recv.at[2], (partner, e))
    drain(acts.at[0], hid_recv.at[0])
    drain(acts.at[1, theirs], hid_recv.at[2])

    def turn(j, carry):
        cols = pl.ds(pl.multiple_of(j * 256, 256), 256)
        for sec in range(2):
            acts_t[cols, sec * (depth // 2) : (sec + 1) * (depth // 2)] = acts[sec, :, cols].T
        return carry

    lax.fori_loop(0, ff // 256, turn, 0)

    def multiply(n, carry):
        @pl.when(n + AHEAD < chunks)
        def _():
            pack(n + AHEAD)

        drain(arrived.at[n, :, :, pl.ds(0, NZ - 1)], z_recv.at[n])
        drain(packed.at[n, 0], z_own.at[n])

        def rows_of(g, inner):
            lhs = acts_t[pl.ds(pl.multiple_of(g * 4 * rows, 4 * rows), 4 * rows), :]
            rhs = arrived[n].reshape(depth, width)
            total = jnp.dot(lhs, rhs, preferred_element_type=jnp.float32)
            result[n, pl.ds(g * 4, 4)] = total.astype(jnp.bfloat16).reshape(4, rows, width)
            return inner

        lax.fori_loop(0, SECTIONS // 4, rows_of, 0)
        place_out = out.at[pair, :, pl.ds(pl.multiple_of(core * half + n * width, width), width)]
        for step in STEPS:
            to = section_at(step)
            remote(result.at[n, to], place_out, out_send, out_recv, (to, e))
        pltpu.make_async_copy(result.at[n, s], place_out, out_own).start()
        return carry

    lax.fori_loop(0, chunks, multiply, 0)

    for i in range(4):
        if i == 0:
            @pl.when(core == 1)
            def _():
                drain(rts.at[0], meta_send.at[0, 0])
                drain(gts.at[0], meta_send.at[0, 1])
                drain(cotb.at[:, 0], cot_send.at[0])
        else:
            drain(rts.at[0], meta_send.at[i, 0])
            drain(gts.at[0], meta_send.at[i, 1])
            drain(cotb.at[:, 0], cot_send.at[i])

    @pl.when(core == 0)
    def _():
        drain(acts.at[0], hid_send.at[0])

    @pl.when(core == 1)
    def _():
        drain(acts.at[1, mine], hid_send.at[0])
        drain(acts.at[1, mine], hid_send.at[1])

    drain(acts.at[1, mine], hid_send.at[2])
    drain(packed.at[:, pl.ds(0, NZ - 1)], z_send)
    drain(result.at[:, pl.ds(0, SECTIONS - 1)], out_send)
    drain(result.at[:, pl.ds(0, 1)], out_own)
    drain(result.at[:, pl.ds(0, SECTIONS - 1)], out_recv)


def local(cotangent, routes, gate_prob, hidden):
    tokens, model = cotangent.shape[1:]
    ff = hidden.shape[5]
    depth = hidden.shape[2] * hidden.shape[3] * hidden.shape[4]
    rows = ff // SECTIONS
    half = model // 2
    chunks = half // CHUNK
    dma = pltpu.SemaphoreType.DMA
    bf16 = jnp.bfloat16
    anywhere = pl.BlockSpec(memory_space=pl.ANY)
    result = pl.pallas_call(
        kernel,
        name="pair_grad",
        out_shape=jax.ShapeDtypeStruct((SECTIONS // 2, rows, model), bf16),
        in_specs=[anywhere] * 4,
        out_specs=anywhere,
        scratch_shapes=[
            pltpu.VMEM((chunks, 4, tokens, CHUNK), bf16),
            pltpu.VMEM((4, 2, tokens), jnp.int32),
            pltpu.VMEM((4, 2, tokens), jnp.float32),
            pltpu.VMEM((4, 2 * NZ * CAP, tokens), bf16),
            pltpu.VMEM((4, 2 * NZ * CAP, tokens), jnp.float32),
            pltpu.VMEM((chunks, NZ, 2, 2, 2 * CAP, CHUNK), bf16),
            pltpu.VMEM((chunks, 2, 2, NZ, 2 * CAP, CHUNK), bf16),
            pltpu.VMEM((2, depth, ff), bf16),
            pltpu.VMEM((ff, 2 * depth), bf16),
            pltpu.VMEM((chunks, SECTIONS, rows, CHUNK), bf16),
            dma((4, 2)), dma((4, 2)), dma((4,)), dma((chunks, 4)), dma((3,)), dma((3,)),
            dma, dma((chunks,)), dma((chunks,)), dma, dma, dma,
        ],
        compiler_params=pltpu.CompilerParams(collective_id=0, has_side_effects=True),
    )(
        cotangent[0],
        routes[0].T,
        gate_prob[0].T,
        hidden.reshape(depth, ff),
    )
    return result[:, None]


def solution(mesh):
    return jax.shard_map(
        local,
        mesh=mesh,
        in_specs=(
            P("section", "expert", None),
            P("section", "expert", None),
            P("section", "expert", None),
            P("section", "expert", None, None, None, None),
        ),
        out_specs=P(None, "expert", "section", None),
        check_vma=False,
    )
```

```python
import functools

import jax
import jax.numpy as jnp
from jax import lax
from jax.experimental import pallas as pl
from jax.experimental.pallas import tpu as pltpu
from jax.sharding import PartitionSpec as P

MESH = pl.DeviceIdType.MESH
NZ = 8
CAP = 16
TOK = 128
BLK = 64
SECTIONS = 16
AHEAD = 4
VMEM_LIMIT = 60_500_000
CHUNK = 256
TAIL = ((0, 128), (128, 128))
STEPS = (
    (0, 1, 0), (1, 0, 0), (0, 3, 1), (1, 2, 0), (0, 2, 0), (1, 1, 1), (0, 0, 1), (1, 3, 0),
    (0, 1, 1), (1, 0, 1), (0, 3, 0), (1, 2, 1), (0, 2, 1), (1, 1, 0), (1, 3, 1),
)
Z_STEPS = (4, 3, 5, 2, 6, 1, 7)


def drain(ref, sem):
    pltpu.make_async_copy(ref, ref, sem).wait()


def kernel(
    cot, routes, gates, hid, out,
    cotb, rts, gts, sel, gain, packed, arrived, acts, acts_t, result,
    meta_send, meta_recv, cot_send, cot_recv, hid_send, hid_recv, z_send, z_recv, z_own, out_send, out_recv, out_own,
):
    chunks, _, _, width = cotb.shape
    ff = acts.shape[2]
    rows = result.shape[2]
    half = chunks * width
    depth = 2 * acts.shape[1]
    s = lax.axis_index("section")
    e = lax.axis_index("expert")
    y_hi, x, core = s // 8, (s // 2) % 4, s % 2
    z, y_lo = e // 2, e % 2
    chip = s // 2
    base = 2 * chip * (1 - core) + (14 - 2 * chip) * core
    pair = 2 * chip * (1 - chip // 4) + (15 - 2 * chip) * (chip // 4)
    other_e = z * 2 + 1 - y_lo
    partner = 2 * chip + 1 - core
    source = core * 2 + y_lo

    def section_at(step):
        a, b, c = step
        return ((y_hi + a) % 2) * 8 + ((x + b) % 4) * 2 + (core + c) % 2

    barrier = pltpu.get_barrier_semaphore()
    peers = [(section_at(step), e) for step in STEPS]
    peers += [(s, ((z + i) % NZ) * 2 + y_lo) for i in range(1, NZ)]
    peers += [(2 * chip, other_e), (2 * chip + 1, other_e), (14 - 2 * chip, other_e), (15 - 2 * chip, other_e)]
    for peer in peers:
        pl.semaphore_signal(barrier, inc=1, device_id=peer, device_id_type=MESH)
    pl.semaphore_wait(barrier, len(peers))

    def remote(src, dst, send, recv, device):
        pltpu.make_async_remote_copy(
            src_ref=src, dst_ref=dst, send_sem=send, recv_sem=recv, device_id=device, device_id_type=MESH
        ).start()

    targets = [(h, f, (base + h, z * 2 + (y_lo + f) % 2)) for h in range(2) for f in range(2)]

    def each_target(to_other, to_self):
        for i, (h, f, device) in enumerate(targets):
            if i == 0:
                @pl.when(core == 0)
                def _():
                    to_self(h)

                @pl.when(core == 1)
                def _():
                    to_other(i, h, device)
            else:
                to_other(i, h, device)

    def send_meta(i, h, device):
        remote(routes, rts.at[source], meta_send.at[i, 0], meta_recv.at[source, 0], device)
        remote(gates, gts.at[source], meta_send.at[i, 1], meta_recv.at[source, 1], device)

    def keep_meta(h):
        pltpu.make_async_copy(routes, rts.at[source], meta_recv.at[source, 0]).start()
        pltpu.make_async_copy(gates, gts.at[source], meta_recv.at[source, 1]).start()

    def send_rows(n):
        def cut(h):
            return cot.at[:, pl.ds(pl.multiple_of(h * half + n * width, width), width)]

        each_target(
            lambda i, h, device: remote(
                cut(h), cotb.at[n, source], cot_send.at[i], cot_recv.at[n, source], device
            ),
            lambda h: pltpu.make_async_copy(cut(h), cotb.at[n, source], cot_recv.at[n, source]).start(),
        )

    each_target(send_meta, keep_meta)
    send_rows(0)
    send_rows(1)

    block = acts.shape[1] // 2

    @pl.when(core == 0)
    def _():
        pltpu.make_async_copy(hid, acts.at[0], hid_recv.at[0]).start()
        remote(hid, acts.at[0], hid_send.at[0], hid_recv.at[0], (partner, e))

    @pl.when(core == 1)
    def _():
        for b in range(2):
            part = pl.ds(b * block, block)
            remote(hid.at[part], acts.at[1, part], hid_send.at[b], hid_recv.at[1], (base + b, e))

    def rest(n, carry):
        send_rows(n)
        return carry

    lax.fori_loop(2, chunks, rest, 0)

    token = lax.broadcasted_iota(jnp.int32, (TOK, TOK), 1)
    row = lax.broadcasted_iota(jnp.int32, (TOK, TOK), 0)
    earlier = jnp.where((row < token) & ((row >> 6) == (token >> 6)), 1.0, 0.0).astype(jnp.bfloat16)
    place = (row & (CAP - 1)).astype(jnp.float32)
    named = lax.broadcasted_iota(jnp.int32, (NZ, TOK), 0) * 2 + y_lo

    def spread(a):
        return jnp.broadcast_to(a[:, None, :], (NZ, CAP, TOK)).reshape(NZ * CAP, TOK)

    def choose(q):
        drain(rts.at[q], meta_recv.at[q, 0])
        drain(gts.at[q], meta_recv.at[q, 1])
        first = rts[q, 0:1, :] == named
        second = rts[q, 1:2, :] == named
        hits = jnp.where(first | second, 1.0, 0.0)
        weight = jnp.where(first, gts[q, 0:1, :], 0.0) + jnp.where(second, gts[q, 1:2, :], 0.0)
        before = jnp.dot(hits.astype(jnp.bfloat16), earlier, preferred_element_type=jnp.float32)
        chosen = (spread(hits) > 0.5) & (spread(before) == place)
        weight = spread(weight)
        for b in range(2):
            mine = chosen & ((token >> 6) == b)
            sel[q, b * TOK : (b + 1) * TOK, :] = jnp.where(mine, 1.0, 0.0).astype(jnp.bfloat16)
            total = jnp.sum(jnp.where(mine, weight, 0.0), axis=1, keepdims=True)
            gain[q, b * TOK : (b + 1) * TOK, :] = jnp.broadcast_to(total, (TOK, TOK))

    def pack_part(n, sec):
        for q in (2 * sec, 2 * sec + 1):
            drain(cotb.at[n, q], cot_recv.at[n, q])
            picked = jnp.dot(sel[q], cotb[n, q], preferred_element_type=jnp.float32)
            scale = jnp.concatenate([gain[q]] * (width // TOK), axis=1)
            slots = (picked * scale).astype(jnp.bfloat16).reshape(2, NZ, CAP, width)
            for b in range(2):
                packed[n, :, sec, b, (q % 2) * CAP : (q % 2 + 1) * CAP, :] = slots[b]

    def ship(n, src, dst, recv, own):
        for i in Z_STEPS:
            to = (z + i) % NZ
            remote(src(to), dst, z_send, recv, (s, to * 2 + y_lo))
        pltpu.make_async_copy(src(z), dst, own).start()

    def pack(n):
        for sec in range(2):
            pack_part(n, sec)
        ship(n, lambda to: packed.at[n, to], arrived.at[n, :, :, z], z_recv.at[n], z_own.at[n])

    def pack_step(n, carry):
        pack(n)
        return carry

    for sec in range(2):
        choose(2 * sec)
        choose(2 * sec + 1)
        pack_part(0, sec)
        ship(0, lambda to: packed.at[0, to, sec], arrived.at[0, sec, :, z], z_recv.at[0], z_own.at[0])

    lax.fori_loop(1, AHEAD, pack_step, 0)

    mine = pl.ds(pl.multiple_of(core * block, block), block)
    theirs = pl.ds(pl.multiple_of((1 - core) * block, block), block)
    drain(acts.at[1, mine], hid_recv.at[1])
    remote(acts.at[1, mine], acts.at[1, mine], hid_send.at[2], hid_recv.at[2], (partner, e))
    drain(acts.at[0], hid_recv.at[0])
    drain(acts.at[1, theirs], hid_recv.at[2])

    def turn(j, carry):
        cols = pl.ds(pl.multiple_of(j * 256, 256), 256)
        for sec in range(2):
            acts_t[cols, sec * (depth // 2) : (sec + 1) * (depth // 2)] = acts[sec, :, cols].T
        return carry

    lax.fori_loop(0, ff // 256, turn, 0)

    last = chunks - 1

    def multiply(n, lanes):
        start, size = lanes

        def rows_of(g, inner):
            lhs = acts_t[pl.ds(pl.multiple_of(g * 4 * rows, 4 * rows), 4 * rows), :]
            rhs = arrived[n, :, :, :, :, start : start + size].reshape(depth, size)
            total = jnp.dot(lhs, rhs, preferred_element_type=jnp.float32)
            result[n, pl.ds(g * 4, 4), :, start : start + size] = total.astype(jnp.bfloat16).reshape(4, rows, size)
            return inner

        lax.fori_loop(0, SECTIONS // 4, rows_of, 0)
        first = pl.multiple_of(core * half + n * width + start, TOK)
        place_out = out.at[pair, :, pl.ds(first, size)]
        for step in STEPS:
            to = section_at(step)
            remote(result.at[n, to, :, start : start + size], place_out, out_send, out_recv, (to, e))
        pltpu.make_async_copy(result.at[n, s, :, start : start + size], place_out, out_own).start()

    def step_on(n, carry):
        @pl.when(n + AHEAD < last)
        def _():
            pack(n + AHEAD)

        @pl.when(n + AHEAD == last)
        def _():
            for sec in range(2):
                pack_part(last, sec)
            for h, (start, size) in enumerate(TAIL):
                cols = slice(start, start + size)
                ship(
                    last, lambda to: packed.at[last, to, :, :, :, cols], arrived.at[last, :, :, z, :, cols],
                    z_recv.at[last + h], z_own.at[last + h],
                )

        drain(arrived.at[n, :, :, pl.ds(0, NZ - 1)], z_recv.at[n])
        drain(packed.at[n, 0], z_own.at[n])
        multiply(n, (0, width))
        return carry

    lax.fori_loop(0, last, step_on, 0)
    for h, (start, size) in enumerate(TAIL):
        cols = slice(start, start + size)
        drain(arrived.at[last, :, :, pl.ds(0, NZ - 1), :, cols], z_recv.at[last + h])
        drain(packed.at[last, 0, :, :, :, cols], z_own.at[last + h])
        multiply(last, (start, size))

    for i in range(4):
        if i == 0:
            @pl.when(core == 1)
            def _():
                drain(rts.at[0], meta_send.at[0, 0])
                drain(gts.at[0], meta_send.at[0, 1])
                drain(cotb.at[:, 0], cot_send.at[0])
        else:
            drain(rts.at[0], meta_send.at[i, 0])
            drain(gts.at[0], meta_send.at[i, 1])
            drain(cotb.at[:, 0], cot_send.at[i])

    @pl.when(core == 0)
    def _():
        drain(acts.at[0], hid_send.at[0])

    @pl.when(core == 1)
    def _():
        drain(acts.at[1, mine], hid_send.at[0])
        drain(acts.at[1, mine], hid_send.at[1])

    drain(acts.at[1, mine], hid_send.at[2])
    drain(packed.at[:, pl.ds(0, NZ - 1)], z_send)
    drain(result.at[:, pl.ds(0, SECTIONS - 1)], out_send)
    drain(result.at[:, pl.ds(0, 1)], out_own)
    drain(result.at[:, pl.ds(0, SECTIONS - 1)], out_recv)


def local(cotangent, routes, gate_prob, hidden):
    tokens, model = cotangent.shape[1:]
    ff = hidden.shape[5]
    depth = hidden.shape[2] * hidden.shape[3] * hidden.shape[4]
    rows = ff // SECTIONS
    half = model // 2
    chunks = half // CHUNK
    dma = pltpu.SemaphoreType.DMA
    bf16 = jnp.bfloat16
    anywhere = pl.BlockSpec(memory_space=pl.ANY)
    result = pl.pallas_call(
        kernel,
        name="pair_grad",
        out_shape=pltpu.VMEM((SECTIONS // 2, rows, model), bf16),
        in_specs=[anywhere] * 4,
        out_specs=pl.BlockSpec(memory_space=pltpu.VMEM),
        scratch_shapes=[
            pltpu.VMEM((chunks, 4, tokens, CHUNK), bf16),
            pltpu.VMEM((4, 2, tokens), jnp.int32),
            pltpu.VMEM((4, 2, tokens), jnp.float32),
            pltpu.VMEM((4, 2 * NZ * CAP, tokens), bf16),
            pltpu.VMEM((4, 2 * NZ * CAP, tokens), jnp.float32),
            pltpu.VMEM((chunks, NZ, 2, 2, 2 * CAP, CHUNK), bf16),
            pltpu.VMEM((chunks, 2, 2, NZ, 2 * CAP, CHUNK), bf16),
            pltpu.VMEM((2, depth, ff), bf16),
            pltpu.VMEM((ff, 2 * depth), bf16),
            pltpu.VMEM((chunks, SECTIONS, rows, CHUNK), bf16),
            dma((4, 2)), dma((4, 2)), dma((4,)), dma((chunks, 4)), dma((3,)), dma((3,)),
            dma, dma((chunks + 1,)), dma((chunks + 1,)), dma, dma, dma,
        ],
        compiler_params=pltpu.CompilerParams(collective_id=0, has_side_effects=True, vmem_limit_bytes=VMEM_LIMIT),
    )(
        cotangent[0],
        routes[0].T,
        gate_prob[0].T,
        hidden.reshape(depth, ff),
    )
    return result[:, None]


def solution(mesh):
    return jax.shard_map(
        local,
        mesh=mesh,
        in_specs=(
            P("section", "expert", None),
            P("section", "expert", None),
            P("section", "expert", None),
            P("section", "expert", None, None, None, None),
        ),
        out_specs=P(None, "expert", "section", None),
        check_vma=False,
    )
```

```python
import functools

import jax
import jax.numpy as jnp
from jax import lax
from jax.experimental import pallas as pl
from jax.experimental.pallas import tpu as pltpu
from jax.sharding import PartitionSpec as P

MESH = pl.DeviceIdType.MESH
NZ = 8
CAP = 16
TOK = 128
BLK = 64
SECTIONS = 16
AHEAD = 4
VMEM_LIMIT = 60_500_000
CHUNK = 256
TAIL = ((0, 128), (128, 128))
STEPS = (
    (0, 1, 0), (1, 0, 0), (0, 3, 1), (1, 2, 0), (0, 2, 0), (1, 1, 1), (0, 0, 1), (1, 3, 0),
    (0, 1, 1), (1, 0, 1), (0, 3, 0), (1, 2, 1), (0, 2, 1), (1, 1, 0), (1, 3, 1),
)
X_STEPS = ((0, 1, 0), (0, 3, 1), (0, 2, 0), (0, 0, 1), (0, 1, 1), (0, 3, 0), (0, 2, 1))
RELAYED = 6
Z_STEPS = (4, 3, 5, 2, 6, 1, 7)


def drain(ref, sem):
    pltpu.make_async_copy(ref, ref, sem).wait()


def kernel(
    cot, routes, gates, hid, out,
    cotb, rts, gts, sel, gain, packed, arrived, acts, acts_t, result, relay,
    meta_send, meta_recv, cot_send, cot_recv, hid_send, hid_recv, z_send, z_recv, z_own,
    y_send, y_recv, out_send, out_recv, out_own,
):
    chunks, _, _, width = cotb.shape
    ff = acts.shape[2]
    rows = result.shape[2]
    half = chunks * width
    depth = 2 * acts.shape[1]
    s = lax.axis_index("section")
    e = lax.axis_index("expert")
    y_hi, x, core = s // 8, (s // 2) % 4, s % 2
    z, y_lo = e // 2, e % 2
    chip = s // 2
    base = 2 * chip * (1 - core) + (14 - 2 * chip) * core

    def pair_of(c):
        return 2 * c * (1 - c // 4) + (15 - 2 * c) * (c // 4)

    pair = pair_of(chip)
    across = ((y_hi + 1) % 2) * 8 + s % 8
    pair_across = pair_of(across // 2)
    other_e = z * 2 + 1 - y_lo
    partner = 2 * chip + 1 - core
    source = core * 2 + y_lo

    def section_at(step):
        a, b, c = step
        return ((y_hi + a) % 2) * 8 + ((x + b) % 4) * 2 + (core + c) % 2

    def cut(n, h):
        return cot.at[:, pl.ds(pl.multiple_of(h * half + n * width, width), width)]

    @pl.when(core == 0)
    def _():
        pltpu.make_async_copy(routes, rts.at[source], meta_recv.at[source, 0]).start()
        pltpu.make_async_copy(gates, gts.at[source], meta_recv.at[source, 1]).start()
        for n in range(chunks):
            pltpu.make_async_copy(cut(n, 0), cotb.at[n, source], cot_recv.at[n, source]).start()
        pltpu.make_async_copy(hid, acts.at[0], hid_recv.at[0]).start()

    barrier = pltpu.get_barrier_semaphore()
    peers = [(section_at(step), e) for step in STEPS]
    peers += [(s, ((z + i) % NZ) * 2 + y_lo) for i in range(1, NZ)]
    peers += [(2 * chip, other_e), (2 * chip + 1, other_e), (14 - 2 * chip, other_e), (15 - 2 * chip, other_e)]
    for peer in peers:
        pl.semaphore_signal(barrier, inc=1, device_id=peer, device_id_type=MESH)
    pl.semaphore_wait(barrier, len(peers))

    def remote(src, dst, send, recv, device):
        pltpu.make_async_remote_copy(
            src_ref=src, dst_ref=dst, send_sem=send, recv_sem=recv, device_id=device, device_id_type=MESH
        ).start()

    targets = [(h, f, (base + h, z * 2 + (y_lo + f) % 2)) for h in range(2) for f in range(2)]

    def each_target(send):
        for i, (h, f, device) in enumerate(targets):
            if i == 0:
                @pl.when(core == 1)
                def _():
                    send(i, h, device)
            else:
                send(i, h, device)

    def send_meta(i, h, device):
        remote(routes, rts.at[source], meta_send.at[i, 0], meta_recv.at[source, 0], device)
        remote(gates, gts.at[source], meta_send.at[i, 1], meta_recv.at[source, 1], device)

    def send_rows(n):
        each_target(
            lambda i, h, device: remote(
                cut(n, h), cotb.at[n, source], cot_send.at[i], cot_recv.at[n, source], device
            )
        )

    each_target(send_meta)
    send_rows(0)
    send_rows(1)

    block = acts.shape[1] // 2

    @pl.when(core == 0)
    def _():
        remote(hid, acts.at[0], hid_send.at[0], hid_recv.at[0], (partner, e))

    @pl.when(core == 1)
    def _():
        for b in range(2):
            part = pl.ds(b * block, block)
            remote(hid.at[part], acts.at[1, part], hid_send.at[b], hid_recv.at[1], (base + b, e))

    def rest(n, carry):
        send_rows(n)
        return carry

    lax.fori_loop(2, chunks, rest, 0)

    token = lax.broadcasted_iota(jnp.int32, (TOK, TOK), 1)
    row = lax.broadcasted_iota(jnp.int32, (TOK, TOK), 0)
    earlier = jnp.where((row < token) & ((row >> 6) == (token >> 6)), 1.0, 0.0).astype(jnp.bfloat16)
    slot = (row & (CAP - 1)).astype(jnp.float32)
    named = lax.broadcasted_iota(jnp.int32, (NZ, TOK), 0) * 2 + y_lo

    def spread(a):
        return jnp.broadcast_to(a[:, None, :], (NZ, CAP, TOK)).reshape(NZ * CAP, TOK)

    def choose(q):
        drain(rts.at[q], meta_recv.at[q, 0])
        drain(gts.at[q], meta_recv.at[q, 1])
        first = rts[q, 0:1, :] == named
        second = rts[q, 1:2, :] == named
        hits = jnp.where(first | second, 1.0, 0.0)
        weight = jnp.where(first, gts[q, 0:1, :], 0.0) + jnp.where(second, gts[q, 1:2, :], 0.0)
        before = jnp.dot(hits.astype(jnp.bfloat16), earlier, preferred_element_type=jnp.float32)
        chosen = (spread(hits) > 0.5) & (spread(before) == slot)
        weight = spread(weight)
        for b in range(2):
            mine = chosen & ((token >> 6) == b)
            sel[q, b * TOK : (b + 1) * TOK, :] = jnp.where(mine, 1.0, 0.0).astype(jnp.bfloat16)
            total = jnp.sum(jnp.where(mine, weight, 0.0), axis=1, keepdims=True)
            gain[q, b * TOK : (b + 1) * TOK, :] = jnp.broadcast_to(total, (TOK, TOK))

    def pack_rows(n, sec, j):
        q = 2 * sec + j
        drain(cotb.at[n, q], cot_recv.at[n, q])
        picked = jnp.dot(sel[q], cotb[n, q], preferred_element_type=jnp.float32)
        scale = jnp.concatenate([gain[q]] * (width // TOK), axis=1)
        slots = (picked * scale).astype(jnp.bfloat16).reshape(2, NZ, CAP, width)
        for b in range(2):
            packed[n, :, sec, b, slots_of(j), :] = slots[b]

    def slots_of(j):
        return pl.ds(pl.multiple_of(j * CAP, CAP), CAP)

    def pack_part(n, sec):
        for j in range(2):
            pack_rows(n, sec, j)

    def ship(n, src, dst, recv, own):
        for i in Z_STEPS:
            to = (z + i) % NZ
            remote(src(to), dst, z_send, recv, (s, to * 2 + y_lo))
        pltpu.make_async_copy(src(z), dst, own).start()

    def pack(n):
        for sec in range(2):
            pack_part(n, sec)
        ship(n, lambda to: packed.at[n, to], arrived.at[n, :, :, z], z_recv.at[n], z_own.at[n])

    def pack_step(n, carry):
        pack(n)
        return carry

    for sec, j in ((0, y_lo), (0, 1 - y_lo), (1, 1 - y_lo), (1, y_lo)):
        choose(2 * sec + j)
        pack_rows(0, sec, j)
        ship(
            0, lambda to: packed.at[0, to, sec, :, slots_of(j)], arrived.at[0, sec, :, z, slots_of(j)],
            z_recv.at[0], z_own.at[0],
        )

    lax.fori_loop(1, AHEAD, pack_step, 0)

    mine = pl.ds(pl.multiple_of(core * block, block), block)
    theirs = pl.ds(pl.multiple_of((1 - core) * block, block), block)
    drain(acts.at[1, mine], hid_recv.at[1])
    remote(acts.at[1, mine], acts.at[1, mine], hid_send.at[2], hid_recv.at[2], (partner, e))
    drain(acts.at[0], hid_recv.at[0])
    drain(acts.at[1, theirs], hid_recv.at[2])

    def turn(j, carry):
        cols = pl.ds(pl.multiple_of(j * 256, 256), 256)
        for sec in range(2):
            acts_t[cols, sec * (depth // 2) : (sec + 1) * (depth // 2)] = acts[sec, :, cols].T
        return carry

    lax.fori_loop(0, ff // 256, turn, 0)

    last = chunks - 1

    def place(p, n, lanes):
        start, size = lanes
        return out.at[p, :, pl.ds(pl.multiple_of(core * half + n * width + start, TOK), size)]

    def multiply(n, lanes):
        start, size = lanes

        def rows_of(g, inner):
            lhs = acts_t[pl.ds(pl.multiple_of(g * 4 * rows, 4 * rows), 4 * rows), :]
            rhs = arrived[n, :, :, :, :, start : start + size].reshape(depth, size)
            total = jnp.dot(lhs, rhs, preferred_element_type=jnp.float32)
            result[n, pl.ds(g * 4, 4), :, start : start + size] = total.astype(jnp.bfloat16).reshape(4, rows, size)
            return inner

        lax.fori_loop(0, SECTIONS // 4, rows_of, 0)

    def send_all(n, lanes):
        start, size = lanes
        for step in STEPS:
            to = section_at(step)
            remote(result.at[n, to, :, start : start + size], place(pair, n, lanes), out_send.at[0], out_recv.at[0], (to, e))
        pltpu.make_async_copy(result.at[n, s, :, start : start + size], place(pair, n, lanes), out_own.at[0]).start()

    def send_near(n, lanes):
        remote(result.at[n, pl.ds(((y_hi + 1) % 2) * 8, 8)], relay.at[n], y_send, y_recv.at[n], (across, e))
        for step in X_STEPS:
            to = section_at(step)
            remote(result.at[n, to], place(pair, n, lanes), out_send.at[1], out_recv.at[1], (to, e))
        pltpu.make_async_copy(result.at[n, s], place(pair, n, lanes), out_own.at[0]).start()

    def pass_on(n, lanes):
        drain(relay.at[n], y_recv.at[n])
        for step in X_STEPS:
            to = section_at(step)
            remote(relay.at[n, to % 8], place(pair_across, n, lanes), out_send.at[2], out_recv.at[2], (to, e))
        pltpu.make_async_copy(relay.at[n, s % 8], place(pair_across, n, lanes), out_own.at[1]).start()

    full = (0, width)

    def step_on(n, carry):
        @pl.when(n + AHEAD < last)
        def _():
            pack(n + AHEAD)

        @pl.when(n + AHEAD == last)
        def _():
            for sec in range(2):
                pack_part(last, sec)
            for h, (start, size) in enumerate(TAIL):
                cols = slice(start, start + size)
                ship(
                    last, lambda to: packed.at[last, to, :, :, :, cols], arrived.at[last, :, :, z, :, cols],
                    z_recv.at[last + h], z_own.at[last + h],
                )

        drain(arrived.at[n, :, :, pl.ds(0, NZ - 1)], z_recv.at[n])
        drain(packed.at[n, 0], z_own.at[n])
        multiply(n, full)

        @pl.when(n < RELAYED)
        def _():
            send_near(n, full)

        @pl.when(n >= RELAYED)
        def _():
            send_all(n, full)

        @pl.when((n >= 1) & (n <= RELAYED))
        def _():
            pass_on(n - 1, full)

        return carry

    lax.fori_loop(0, last, step_on, 0)
    for h, (start, size) in enumerate(TAIL):
        cols = slice(start, start + size)
        drain(arrived.at[last, :, :, pl.ds(0, NZ - 1), :, cols], z_recv.at[last + h])
        drain(packed.at[last, 0, :, :, :, cols], z_own.at[last + h])
        multiply(last, (start, size))
        send_all(last, (start, size))

    for i in range(4):
        if i == 0:
            @pl.when(core == 1)
            def _():
                drain(rts.at[0], meta_send.at[0, 0])
                drain(gts.at[0], meta_send.at[0, 1])
                drain(cotb.at[:, 0], cot_send.at[0])
        else:
            drain(rts.at[0], meta_send.at[i, 0])
            drain(gts.at[0], meta_send.at[i, 1])
            drain(cotb.at[:, 0], cot_send.at[i])

    @pl.when(core == 0)
    def _():
        drain(acts.at[0], hid_send.at[0])

    @pl.when(core == 1)
    def _():
        drain(acts.at[1, mine], hid_send.at[0])
        drain(acts.at[1, mine], hid_send.at[1])

    drain(acts.at[1, mine], hid_send.at[2])
    drain(packed.at[:, pl.ds(0, NZ - 1)], z_send)
    direct = result.at[pl.ds(RELAYED, chunks - RELAYED), pl.ds(0, SECTIONS - 1)]
    near = result.at[pl.ds(0, RELAYED), pl.ds(0, len(X_STEPS))]
    drain(relay, y_send)
    for sems in (out_send, out_recv):
        drain(direct, sems.at[0])
        drain(near, sems.at[1])
        drain(near, sems.at[2])
    drain(result.at[:, pl.ds(0, 1)], out_own.at[0])
    drain(relay.at[:, pl.ds(0, 1)], out_own.at[1])


def local(cotangent, routes, gate_prob, hidden):
    tokens, model = cotangent.shape[1:]
    ff = hidden.shape[5]
    depth = hidden.shape[2] * hidden.shape[3] * hidden.shape[4]
    rows = ff // SECTIONS
    half = model // 2
    chunks = half // CHUNK
    dma = pltpu.SemaphoreType.DMA
    bf16 = jnp.bfloat16
    anywhere = pl.BlockSpec(memory_space=pl.ANY)
    result = pl.pallas_call(
        kernel,
        name="pair_grad",
        out_shape=pltpu.VMEM((SECTIONS // 2, rows, model), bf16),
        in_specs=[anywhere] * 4,
        out_specs=pl.BlockSpec(memory_space=pltpu.VMEM),
        scratch_shapes=[
            pltpu.VMEM((chunks, 4, tokens, CHUNK), bf16),
            pltpu.VMEM((4, 2, tokens), jnp.int32),
            pltpu.VMEM((4, 2, tokens), jnp.float32),
            pltpu.VMEM((4, 2 * NZ * CAP, tokens), bf16),
            pltpu.VMEM((4, 2 * NZ * CAP, tokens), jnp.float32),
            pltpu.VMEM((chunks, NZ, 2, 2, 2 * CAP, CHUNK), bf16),
            pltpu.VMEM((chunks, 2, 2, NZ, 2 * CAP, CHUNK), bf16),
            pltpu.VMEM((2, depth, ff), bf16),
            pltpu.VMEM((ff, 2 * depth), bf16),
            pltpu.VMEM((chunks, SECTIONS, rows, CHUNK), bf16),
            pltpu.VMEM((RELAYED, SECTIONS // 2, rows, CHUNK), bf16),
            dma((4, 2)), dma((4, 2)), dma((4,)), dma((chunks, 4)), dma((3,)), dma((3,)),
            dma, dma((chunks + 1,)), dma((chunks + 1,)),
            dma, dma((RELAYED,)), dma((3,)), dma((3,)), dma((2,)),
        ],
        compiler_params=pltpu.CompilerParams(collective_id=0, has_side_effects=True, vmem_limit_bytes=VMEM_LIMIT),
    )(
        cotangent[0],
        routes[0].T,
        gate_prob[0].T,
        hidden.reshape(depth, ff),
    )
    return result[:, None]


def solution(mesh):
    return jax.shard_map(
        local,
        mesh=mesh,
        in_specs=(
            P("section", "expert", None),
            P("section", "expert", None),
            P("section", "expert", None),
            P("section", "expert", None, None, None, None),
        ),
        out_specs=P(None, "expert", "section", None),
        check_vma=False,
    )
```

```python
import functools

import jax
import jax.numpy as jnp
from jax import lax
from jax.experimental import pallas as pl
from jax.experimental.pallas import tpu as pltpu
from jax.sharding import PartitionSpec as P

MESH = pl.DeviceIdType.MESH
NZ = 8
CAP = 16
TOK = 128
BLK = 64
SECTIONS = 16
AHEAD = 4
VMEM_LIMIT = 60_500_000
CHUNK = 256
EARLY = 4
TAIL = ((0, 128), (128, 128))
STEPS = (
    (0, 1, 0), (1, 0, 0), (0, 3, 1), (1, 2, 0), (0, 2, 0), (1, 1, 1), (0, 0, 1), (1, 3, 0),
    (0, 1, 1), (1, 0, 1), (0, 3, 0), (1, 2, 1), (0, 2, 1), (1, 1, 0), (1, 3, 1),
)
Z_STEPS = (4, 3, 5, 2, 6, 1, 7)


def drain(ref, sem):
    pltpu.make_async_copy(ref, ref, sem).wait()


def kernel(
    cot, routes, gates, hid, out,
    cotb, rts, gts, sel, gain, packed, arrived, acts, acts_t, result,
    meta_send, meta_recv, cot_send, cot_recv, hid_send, hid_recv, z_send, z_recv, z_own, out_send, out_recv, out_own,
):
    chunks, _, _, width = cotb.shape
    ff = acts.shape[2]
    rows = result.shape[2]
    half = chunks * width
    depth = 2 * acts.shape[1]
    s = lax.axis_index("section")
    e = lax.axis_index("expert")
    y_hi, x, core = s // 8, (s // 2) % 4, s % 2
    z, y_lo = e // 2, e % 2
    chip = s // 2
    base = 2 * chip * (1 - core) + (14 - 2 * chip) * core
    pair = 2 * chip * (1 - chip // 4) + (15 - 2 * chip) * (chip // 4)
    other_e = z * 2 + 1 - y_lo
    partner = 2 * chip + 1 - core
    source = core * 2 + y_lo

    def section_at(step):
        a, b, c = step
        return ((y_hi + a) % 2) * 8 + ((x + b) % 4) * 2 + (core + c) % 2

    barrier = pltpu.get_barrier_semaphore()
    peers = [(section_at(step), e) for step in STEPS]
    peers += [(s, ((z + i) % NZ) * 2 + y_lo) for i in range(1, NZ)]
    peers += [(2 * chip, other_e), (2 * chip + 1, other_e), (14 - 2 * chip, other_e), (15 - 2 * chip, other_e)]
    for peer in peers:
        pl.semaphore_signal(barrier, inc=1, device_id=peer, device_id_type=MESH)
    pl.semaphore_wait(barrier, len(peers))

    def remote(src, dst, send, recv, device):
        pltpu.make_async_remote_copy(
            src_ref=src, dst_ref=dst, send_sem=send, recv_sem=recv, device_id=device, device_id_type=MESH
        ).start()

    targets = [(h, f, (base + h, z * 2 + (y_lo + f) % 2)) for h in range(2) for f in range(2)]

    def each_target(to_other, to_self):
        for i, (h, f, device) in enumerate(targets):
            if i == 0:
                @pl.when(core == 0)
                def _():
                    to_self(h)

                @pl.when(core == 1)
                def _():
                    to_other(i, h, device)
            else:
                to_other(i, h, device)

    def send_meta(i, h, device):
        remote(routes, rts.at[source], meta_send.at[i, 0], meta_recv.at[source, 0], device)
        remote(gates, gts.at[source], meta_send.at[i, 1], meta_recv.at[source, 1], device)

    def keep_meta(h):
        pltpu.make_async_copy(routes, rts.at[source], meta_recv.at[source, 0]).start()
        pltpu.make_async_copy(gates, gts.at[source], meta_recv.at[source, 1]).start()

    def send_rows(n):
        def cut(h):
            return cot.at[:, pl.ds(pl.multiple_of(h * half + n * width, width), width)]

        each_target(
            lambda i, h, device: remote(
                cut(h), cotb.at[n, source], cot_send.at[i], cot_recv.at[n, source], device
            ),
            lambda h: pltpu.make_async_copy(cut(h), cotb.at[n, source], cot_recv.at[n, source]).start(),
        )

    each_target(send_meta, keep_meta)
    def rest(n, carry):
        send_rows(n)
        return carry

    lax.fori_loop(0, EARLY, rest, 0)

    block = acts.shape[1] // 2

    @pl.when(core == 0)
    def _():
        pltpu.make_async_copy(hid, acts.at[0], hid_recv.at[0]).start()
        remote(hid, acts.at[0], hid_send.at[0], hid_recv.at[0], (partner, e))

    @pl.when(core == 1)
    def _():
        for b in range(2):
            part = pl.ds(b * block, block)
            remote(hid.at[part], acts.at[1, part], hid_send.at[b], hid_recv.at[1], (base + b, e))

    lax.fori_loop(EARLY, chunks, rest, 0)

    token = lax.broadcasted_iota(jnp.int32, (TOK, TOK), 1)
    row = lax.broadcasted_iota(jnp.int32, (TOK, TOK), 0)
    earlier = jnp.where((row < token) & ((row >> 6) == (token >> 6)), 1.0, 0.0).astype(jnp.bfloat16)
    place = (row & (CAP - 1)).astype(jnp.float32)
    named = lax.broadcasted_iota(jnp.int32, (NZ, TOK), 0) * 2 + y_lo

    def spread(a):
        return jnp.broadcast_to(a[:, None, :], (NZ, CAP, TOK)).reshape(NZ * CAP, TOK)

    def choose(q):
        drain(rts.at[q], meta_recv.at[q, 0])
        drain(gts.at[q], meta_recv.at[q, 1])
        first = rts[q, 0:1, :] == named
        second = rts[q, 1:2, :] == named
        hits = jnp.where(first | second, 1.0, 0.0)
        weight = jnp.where(first, gts[q, 0:1, :], 0.0) + jnp.where(second, gts[q, 1:2, :], 0.0)
        before = jnp.dot(hits.astype(jnp.bfloat16), earlier, preferred_element_type=jnp.float32)
        chosen = (spread(hits) > 0.5) & (spread(before) == place)
        weight = spread(weight)
        for b in range(2):
            mine = chosen & ((token >> 6) == b)
            sel[q, b * TOK : (b + 1) * TOK, :] = jnp.where(mine, 1.0, 0.0).astype(jnp.bfloat16)
            total = jnp.sum(jnp.where(mine, weight, 0.0), axis=1, keepdims=True)
            gain[q, b * TOK : (b + 1) * TOK, :] = jnp.broadcast_to(total, (TOK, TOK))

    def pack_part(n, sec):
        for q in (2 * sec, 2 * sec + 1):
            drain(cotb.at[n, q], cot_recv.at[n, q])
            picked = jnp.dot(sel[q], cotb[n, q], preferred_element_type=jnp.float32)
            scale = jnp.concatenate([gain[q]] * (width // TOK), axis=1)
            slots = (picked * scale).astype(jnp.bfloat16).reshape(2, NZ, CAP, width)
            for b in range(2):
                packed[n, :, sec, b, (q % 2) * CAP : (q % 2 + 1) * CAP, :] = slots[b]

    def ship(n, src, dst, recv, own):
        for i in Z_STEPS:
            to = (z + i) % NZ
            remote(src(to), dst, z_send, recv, (s, to * 2 + y_lo))
        pltpu.make_async_copy(src(z), dst, own).start()

    def pack(n):
        for sec in range(2):
            pack_part(n, sec)
        ship(n, lambda to: packed.at[n, to], arrived.at[n, :, :, z], z_recv.at[n], z_own.at[n])

    def pack_step(n, carry):
        pack(n)
        return carry

    for sec in range(2):
        choose(2 * sec)
        choose(2 * sec + 1)
        pack_part(0, sec)
        ship(0, lambda to: packed.at[0, to, sec], arrived.at[0, sec, :, z], z_recv.at[0], z_own.at[0])

    lax.fori_loop(1, AHEAD, pack_step, 0)

    mine = pl.ds(pl.multiple_of(core * block, block), block)
    theirs = pl.ds(pl.multiple_of((1 - core) * block, block), block)
    drain(acts.at[1, mine], hid_recv.at[1])
    remote(acts.at[1, mine], acts.at[1, mine], hid_send.at[2], hid_recv.at[2], (partner, e))
    drain(acts.at[0], hid_recv.at[0])
    drain(acts.at[1, theirs], hid_recv.at[2])

    def turn(j, carry):
        cols = pl.ds(pl.multiple_of(j * 256, 256), 256)
        for sec in range(2):
            acts_t[cols, sec * (depth // 2) : (sec + 1) * (depth // 2)] = acts[sec, :, cols].T
        return carry

    lax.fori_loop(0, ff // 256, turn, 0)

    last = chunks - 1

    def multiply(n, lanes):
        start, size = lanes

        def rows_of(g, inner):
            lhs = acts_t[pl.ds(pl.multiple_of(g * 4 * rows, 4 * rows), 4 * rows), :]
            rhs = arrived[n, :, :, :, :, start : start + size].reshape(depth, size)
            total = jnp.dot(lhs, rhs, preferred_element_type=jnp.float32)
            result[n, pl.ds(g * 4, 4), :, start : start + size] = total.astype(jnp.bfloat16).reshape(4, rows, size)
            return inner

        lax.fori_loop(0, SECTIONS // 4, rows_of, 0)
        first = pl.multiple_of(core * half + n * width + start, TOK)
        place_out = out.at[pair, :, pl.ds(first, size)]
        for step in STEPS:
            to = section_at(step)
            remote(result.at[n, to, :, start : start + size], place_out, out_send, out_recv, (to, e))
        pltpu.make_async_copy(result.at[n, s, :, start : start + size], place_out, out_own).start()

    def step_on(n, carry):
        @pl.when(n + AHEAD < last)
        def _():
            pack(n + AHEAD)

        @pl.when(n + AHEAD == last)
        def _():
            for sec in range(2):
                pack_part(last, sec)
            for h, (start, size) in enumerate(TAIL):
                cols = slice(start, start + size)
                ship(
                    last, lambda to: packed.at[last, to, :, :, :, cols], arrived.at[last, :, :, z, :, cols],
                    z_recv.at[last + h], z_own.at[last + h],
                )

        drain(arrived.at[n, :, :, pl.ds(0, NZ - 1)], z_recv.at[n])
        drain(packed.at[n, 0], z_own.at[n])
        multiply(n, (0, width))
        return carry

    lax.fori_loop(0, last, step_on, 0)
    for h, (start, size) in enumerate(TAIL):
        cols = slice(start, start + size)
        drain(arrived.at[last, :, :, pl.ds(0, NZ - 1), :, cols], z_recv.at[last + h])
        drain(packed.at[last, 0, :, :, :, cols], z_own.at[last + h])
        multiply(last, (start, size))

    for i in range(4):
        if i == 0:
            @pl.when(core == 1)
            def _():
                drain(rts.at[0], meta_send.at[0, 0])
                drain(gts.at[0], meta_send.at[0, 1])
                drain(cotb.at[:, 0], cot_send.at[0])
        else:
            drain(rts.at[0], meta_send.at[i, 0])
            drain(gts.at[0], meta_send.at[i, 1])
            drain(cotb.at[:, 0], cot_send.at[i])

    @pl.when(core == 0)
    def _():
        drain(acts.at[0], hid_send.at[0])

    @pl.when(core == 1)
    def _():
        drain(acts.at[1, mine], hid_send.at[0])
        drain(acts.at[1, mine], hid_send.at[1])

    drain(acts.at[1, mine], hid_send.at[2])
    drain(packed.at[:, pl.ds(0, NZ - 1)], z_send)
    drain(result.at[:, pl.ds(0, SECTIONS - 1)], out_send)
    drain(result.at[:, pl.ds(0, 1)], out_own)
    drain(result.at[:, pl.ds(0, SECTIONS - 1)], out_recv)


def local(cotangent, routes, gate_prob, hidden):
    tokens, model = cotangent.shape[1:]
    ff = hidden.shape[5]
    depth = hidden.shape[2] * hidden.shape[3] * hidden.shape[4]
    rows = ff // SECTIONS
    half = model // 2
    chunks = half // CHUNK
    dma = pltpu.SemaphoreType.DMA
    bf16 = jnp.bfloat16
    anywhere = pl.BlockSpec(memory_space=pl.ANY)
    result = pl.pallas_call(
        kernel,
        name="pair_grad",
        out_shape=pltpu.VMEM((SECTIONS // 2, rows, model), bf16),
        in_specs=[anywhere] * 4,
        out_specs=pl.BlockSpec(memory_space=pltpu.VMEM),
        scratch_shapes=[
            pltpu.VMEM((chunks, 4, tokens, CHUNK), bf16),
            pltpu.VMEM((4, 2, tokens), jnp.int32),
            pltpu.VMEM((4, 2, tokens), jnp.float32),
            pltpu.VMEM((4, 2 * NZ * CAP, tokens), bf16),
            pltpu.VMEM((4, 2 * NZ * CAP, tokens), jnp.float32),
            pltpu.VMEM((chunks, NZ, 2, 2, 2 * CAP, CHUNK), bf16),
            pltpu.VMEM((chunks, 2, 2, NZ, 2 * CAP, CHUNK), bf16),
            pltpu.VMEM((2, depth, ff), bf16),
            pltpu.VMEM((ff, 2 * depth), bf16),
            pltpu.VMEM((chunks, SECTIONS, rows, CHUNK), bf16),
            dma((4, 2)), dma((4, 2)), dma((4,)), dma((chunks, 4)), dma((3,)), dma((3,)),
            dma, dma((chunks + 1,)), dma((chunks + 1,)), dma, dma, dma,
        ],
        compiler_params=pltpu.CompilerParams(collective_id=0, has_side_effects=True, vmem_limit_bytes=VMEM_LIMIT),
    )(
        cotangent[0],
        routes[0].T,
        gate_prob[0].T,
        hidden.reshape(depth, ff),
    )
    return result[:, None]


def solution(mesh):
    return jax.shard_map(
        local,
        mesh=mesh,
        in_specs=(
            P("section", "expert", None),
            P("section", "expert", None),
            P("section", "expert", None),
            P("section", "expert", None, None, None, None),
        ),
        out_specs=P(None, "expert", "section", None),
        check_vma=False,
    )
```

```python
import functools

import jax
import jax.numpy as jnp
from jax import lax
from jax.experimental import pallas as pl
from jax.experimental.pallas import tpu as pltpu
from jax.sharding import PartitionSpec as P

MESH = pl.DeviceIdType.MESH
NZ = 8
CAP = 16
TOK = 128
BLK = 64
SECTIONS = 16
AHEAD = 5
VMEM_LIMIT = 60_500_000
CHUNK = 256
EARLY = 5
TAIL = ((0, 128), (128, 128))
STEPS = (
    (0, 1, 0), (1, 0, 0), (0, 3, 1), (1, 2, 0), (0, 2, 0), (1, 1, 1), (0, 0, 1), (1, 3, 0),
    (0, 1, 1), (1, 0, 1), (0, 3, 0), (1, 2, 1), (0, 2, 1), (1, 1, 0), (1, 3, 1),
)
Z_STEPS = (4, 3, 5, 2, 6, 1, 7)


def drain(ref, sem):
    pltpu.make_async_copy(ref, ref, sem).wait()


def kernel(
    cot, routes, gates, hid, out,
    cotb, rts, gts, sel, gain, packed, arrived, acts, acts_t, result,
    meta_send, meta_recv, cot_send, cot_recv, hid_send, hid_recv, z_send, z_recv, z_own, out_send, out_recv, out_own,
):
    chunks, _, _, width = cotb.shape
    ff = acts.shape[2]
    rows = result.shape[2]
    half = chunks * width
    depth = 2 * acts.shape[1]
    s = lax.axis_index("section")
    e = lax.axis_index("expert")
    y_hi, x, core = s // 8, (s // 2) % 4, s % 2
    z, y_lo = e // 2, e % 2
    chip = s // 2
    base = 2 * chip * (1 - core) + (14 - 2 * chip) * core
    pair = 2 * chip * (1 - chip // 4) + (15 - 2 * chip) * (chip // 4)
    other_e = z * 2 + 1 - y_lo
    partner = 2 * chip + 1 - core
    source = core * 2 + y_lo

    def section_at(step):
        a, b, c = step
        return ((y_hi + a) % 2) * 8 + ((x + b) % 4) * 2 + (core + c) % 2

    barrier = pltpu.get_barrier_semaphore()
    peers = [(section_at(step), e) for step in STEPS]
    peers += [(s, ((z + i) % NZ) * 2 + y_lo) for i in range(1, NZ)]
    peers += [(2 * chip, other_e), (2 * chip + 1, other_e), (14 - 2 * chip, other_e), (15 - 2 * chip, other_e)]
    for peer in peers:
        pl.semaphore_signal(barrier, inc=1, device_id=peer, device_id_type=MESH)
    pl.semaphore_wait(barrier, len(peers))

    def remote(src, dst, send, recv, device):
        pltpu.make_async_remote_copy(
            src_ref=src, dst_ref=dst, send_sem=send, recv_sem=recv, device_id=device, device_id_type=MESH
        ).start()

    targets = [(h, f, (base + h, z * 2 + (y_lo + f) % 2)) for h in range(2) for f in range(2)]

    def each_target(to_other, to_self):
        for i, (h, f, device) in enumerate(targets):
            if i == 0:
                @pl.when(core == 0)
                def _():
                    to_self(h)

                @pl.when(core == 1)
                def _():
                    to_other(i, h, device)
            else:
                to_other(i, h, device)

    def send_meta(i, h, device):
        remote(routes, rts.at[source], meta_send.at[i, 0], meta_recv.at[source, 0], device)
        remote(gates, gts.at[source], meta_send.at[i, 1], meta_recv.at[source, 1], device)

    def keep_meta(h):
        pltpu.make_async_copy(routes, rts.at[source], meta_recv.at[source, 0]).start()
        pltpu.make_async_copy(gates, gts.at[source], meta_recv.at[source, 1]).start()

    def send_rows(n):
        def cut(h):
            return cot.at[:, pl.ds(pl.multiple_of(h * half + n * width, width), width)]

        each_target(
            lambda i, h, device: remote(
                cut(h), cotb.at[n, source], cot_send.at[i], cot_recv.at[n, source], device
            ),
            lambda h: pltpu.make_async_copy(cut(h), cotb.at[n, source], cot_recv.at[n, source]).start(),
        )

    each_target(send_meta, keep_meta)
    def rest(n, carry):
        send_rows(n)
        return carry

    lax.fori_loop(0, EARLY, rest, 0)

    block = acts.shape[1] // 2

    @pl.when(core == 0)
    def _():
        pltpu.make_async_copy(hid, acts.at[0], hid_recv.at[0]).start()
        remote(hid, acts.at[0], hid_send.at[0], hid_recv.at[0], (partner, e))

    @pl.when(core == 1)
    def _():
        for b in range(2):
            part = pl.ds(b * block, block)
            remote(hid.at[part], acts.at[1, part], hid_send.at[b], hid_recv.at[1], (base + b, e))

    lax.fori_loop(EARLY, chunks, rest, 0)

    token = lax.broadcasted_iota(jnp.int32, (TOK, TOK), 1)
    row = lax.broadcasted_iota(jnp.int32, (TOK, TOK), 0)
    earlier = jnp.where((row < token) & ((row >> 6) == (token >> 6)), 1.0, 0.0).astype(jnp.bfloat16)
    place = (row & (CAP - 1)).astype(jnp.float32)
    named = lax.broadcasted_iota(jnp.int32, (NZ, TOK), 0) * 2 + y_lo

    def spread(a):
        return jnp.broadcast_to(a[:, None, :], (NZ, CAP, TOK)).reshape(NZ * CAP, TOK)

    def choose(q):
        drain(rts.at[q], meta_recv.at[q, 0])
        drain(gts.at[q], meta_recv.at[q, 1])
        first = rts[q, 0:1, :] == named
        second = rts[q, 1:2, :] == named
        hits = jnp.where(first | second, 1.0, 0.0)
        weight = jnp.where(first, gts[q, 0:1, :], 0.0) + jnp.where(second, gts[q, 1:2, :], 0.0)
        before = jnp.dot(hits.astype(jnp.bfloat16), earlier, preferred_element_type=jnp.float32)
        chosen = (spread(hits) > 0.5) & (spread(before) == place)
        weight = spread(weight)
        for b in range(2):
            mine = chosen & ((token >> 6) == b)
            sel[q, b * TOK : (b + 1) * TOK, :] = jnp.where(mine, 1.0, 0.0).astype(jnp.bfloat16)
            total = jnp.sum(jnp.where(mine, weight, 0.0), axis=1, keepdims=True)
            gain[q, b * TOK : (b + 1) * TOK, :] = jnp.broadcast_to(total, (TOK, TOK))

    def pack_part(n, sec):
        for q in (2 * sec, 2 * sec + 1):
            drain(cotb.at[n, q], cot_recv.at[n, q])
            picked = jnp.dot(sel[q], cotb[n, q], preferred_element_type=jnp.float32)
            scale = jnp.concatenate([gain[q]] * (width // TOK), axis=1)
            slots = (picked * scale).astype(jnp.bfloat16).reshape(2, NZ, CAP, width)
            for b in range(2):
                packed[n, :, sec, b, (q % 2) * CAP : (q % 2 + 1) * CAP, :] = slots[b]

    def ship(n, src, dst, recv, own):
        for i in Z_STEPS:
            to = (z + i) % NZ
            remote(src(to), dst, z_send, recv, (s, to * 2 + y_lo))
        pltpu.make_async_copy(src(z), dst, own).start()

    def pack(n):
        for sec in range(2):
            pack_part(n, sec)
        ship(n, lambda to: packed.at[n, to], arrived.at[n, :, :, z], z_recv.at[n], z_own.at[n])

    def pack_step(n, carry):
        pack(n)
        return carry

    for sec in range(2):
        choose(2 * sec)
        choose(2 * sec + 1)
        pack_part(0, sec)
        ship(0, lambda to: packed.at[0, to, sec], arrived.at[0, sec, :, z], z_recv.at[0], z_own.at[0])

    lax.fori_loop(1, AHEAD, pack_step, 0)

    mine = pl.ds(pl.multiple_of(core * block, block), block)
    theirs = pl.ds(pl.multiple_of((1 - core) * block, block), block)
    drain(acts.at[1, mine], hid_recv.at[1])
    remote(acts.at[1, mine], acts.at[1, mine], hid_send.at[2], hid_recv.at[2], (partner, e))
    drain(acts.at[0], hid_recv.at[0])
    drain(acts.at[1, theirs], hid_recv.at[2])

    def turn(j, carry):
        cols = pl.ds(pl.multiple_of(j * 256, 256), 256)
        for sec in range(2):
            acts_t[cols, sec * (depth // 2) : (sec + 1) * (depth // 2)] = acts[sec, :, cols].T
        return carry

    lax.fori_loop(0, ff // 256, turn, 0)

    last = chunks - 1

    def multiply(n, lanes):
        start, size = lanes

        def rows_of(g, inner):
            lhs = acts_t[pl.ds(pl.multiple_of(g * 4 * rows, 4 * rows), 4 * rows), :]
            rhs = arrived[n, :, :, :, :, start : start + size].reshape(depth, size)
            total = jnp.dot(lhs, rhs, preferred_element_type=jnp.float32)
            result[n, pl.ds(g * 4, 4), :, start : start + size] = total.astype(jnp.bfloat16).reshape(4, rows, size)
            return inner

        lax.fori_loop(0, SECTIONS // 4, rows_of, 0)
        first = pl.multiple_of(core * half + n * width + start, TOK)
        place_out = out.at[pair, :, pl.ds(first, size)]
        for step in STEPS:
            to = section_at(step)
            remote(result.at[n, to, :, start : start + size], place_out, out_send, out_recv, (to, e))
        pltpu.make_async_copy(result.at[n, s, :, start : start + size], place_out, out_own).start()

    def step_on(n, carry):
        @pl.when(n + AHEAD < last)
        def _():
            pack(n + AHEAD)

        @pl.when(n + AHEAD == last)
        def _():
            for sec in range(2):
                pack_part(last, sec)
            for h, (start, size) in enumerate(TAIL):
                cols = slice(start, start + size)
                ship(
                    last, lambda to: packed.at[last, to, :, :, :, cols], arrived.at[last, :, :, z, :, cols],
                    z_recv.at[last + h], z_own.at[last + h],
                )

        drain(arrived.at[n, :, :, pl.ds(0, NZ - 1)], z_recv.at[n])
        drain(packed.at[n, 0], z_own.at[n])
        multiply(n, (0, width))
        return carry

    lax.fori_loop(0, last, step_on, 0)
    for h, (start, size) in enumerate(TAIL):
        cols = slice(start, start + size)
        drain(arrived.at[last, :, :, pl.ds(0, NZ - 1), :, cols], z_recv.at[last + h])
        drain(packed.at[last, 0, :, :, :, cols], z_own.at[last + h])
        multiply(last, (start, size))

    for i in range(4):
        if i == 0:
            @pl.when(core == 1)
            def _():
                drain(rts.at[0], meta_send.at[0, 0])
                drain(gts.at[0], meta_send.at[0, 1])
                drain(cotb.at[:, 0], cot_send.at[0])
        else:
            drain(rts.at[0], meta_send.at[i, 0])
            drain(gts.at[0], meta_send.at[i, 1])
            drain(cotb.at[:, 0], cot_send.at[i])

    @pl.when(core == 0)
    def _():
        drain(acts.at[0], hid_send.at[0])

    @pl.when(core == 1)
    def _():
        drain(acts.at[1, mine], hid_send.at[0])
        drain(acts.at[1, mine], hid_send.at[1])

    drain(acts.at[1, mine], hid_send.at[2])
    drain(packed.at[:, pl.ds(0, NZ - 1)], z_send)
    drain(result.at[:, pl.ds(0, SECTIONS - 1)], out_send)
    drain(result.at[:, pl.ds(0, 1)], out_own)
    drain(result.at[:, pl.ds(0, SECTIONS - 1)], out_recv)


def local(cotangent, routes, gate_prob, hidden):
    tokens, model = cotangent.shape[1:]
    ff = hidden.shape[5]
    depth = hidden.shape[2] * hidden.shape[3] * hidden.shape[4]
    rows = ff // SECTIONS
    half = model // 2
    chunks = half // CHUNK
    dma = pltpu.SemaphoreType.DMA
    bf16 = jnp.bfloat16
    anywhere = pl.BlockSpec(memory_space=pl.ANY)
    result = pl.pallas_call(
        kernel,
        name="pair_grad",
        out_shape=pltpu.VMEM((SECTIONS // 2, rows, model), bf16),
        in_specs=[anywhere] * 4,
        out_specs=pl.BlockSpec(memory_space=pltpu.VMEM),
        scratch_shapes=[
            pltpu.VMEM((chunks, 4, tokens, CHUNK), bf16),
            pltpu.VMEM((4, 2, tokens), jnp.int32),
            pltpu.VMEM((4, 2, tokens), jnp.float32),
            pltpu.VMEM((4, 2 * NZ * CAP, tokens), bf16),
            pltpu.VMEM((4, 2 * NZ * CAP, tokens), jnp.float32),
            pltpu.VMEM((chunks, NZ, 2, 2, 2 * CAP, CHUNK), bf16),
            pltpu.VMEM((chunks, 2, 2, NZ, 2 * CAP, CHUNK), bf16),
            pltpu.VMEM((2, depth, ff), bf16),
            pltpu.VMEM((ff, 2 * depth), bf16),
            pltpu.VMEM((chunks, SECTIONS, rows, CHUNK), bf16),
            dma((4, 2)), dma((4, 2)), dma((4,)), dma((chunks, 4)), dma((3,)), dma((3,)),
            dma, dma((chunks + 1,)), dma((chunks + 1,)), dma, dma, dma,
        ],
        compiler_params=pltpu.CompilerParams(collective_id=0, has_side_effects=True, vmem_limit_bytes=VMEM_LIMIT),
    )(
        cotangent[0],
        routes[0].T,
        gate_prob[0].T,
        hidden.reshape(depth, ff),
    )
    return result[:, None]


def solution(mesh):
    return jax.shard_map(
        local,
        mesh=mesh,
        in_specs=(
            P("section", "expert", None),
            P("section", "expert", None),
            P("section", "expert", None),
            P("section", "expert", None, None, None, None),
        ),
        out_specs=P(None, "expert", "section", None),
        check_vma=False,
    )
```
